256 devices in a mesh: gx: 8 (over y, x_lo), gy: 4 (over x_hi, core), gz: 8 (over z).
Axes of the slice: x: 4 (x_hi: 2, x_lo: 2; x = x_hi * 2 + x_lo), y: 4, z: 8, core: 2. Of those that a mesh axis runs over, the one named last changes fastest.
Arguments:
- tensor_blocks: bfloat16 [8, 4, 8, 3, 128, 128, 128], P('gx', 'gy', 'gz'), may hold values from 0 to 3
- fiber_mask: int32 [8, 4, 8, 3, 128, 128], P('gx', 'gy', 'gz'), may hold values 0 or 1
- block_coords: int32 [8, 4, 8, 3, 3], P('gx', 'gy', 'gz'), may hold values from 0 to 7, as said below
- block_counts: int32 [8, 4, 8], P('gx', 'gy', 'gz'), may hold values from 0 to 3, as said below
- factor_a: bfloat16 [8, 512, 256], P('gx', ('gy', 'gz')), may hold values from -0.59765625 to 0.59765625
- factor_b: bfloat16 [4, 1024, 256], P('gy', ('gx', 'gz')), may hold values from -0.59765625 to 0.59765625
- factor_c: bfloat16 [8, 512, 256], P('gz', ('gx', 'gy')), may hold values from -0.59765625 to 0.59765625
Outputs:
- grad_a: float32 [8, 512, 256], P('gx', ('gy', 'gz'))
- grad_b: float32 [4, 1024, 256], P('gy', ('gx', 'gz'))
- grad_c: float32 [8, 512, 256], P('gz', ('gx', 'gy'))
The draws below stay inside these ranges and needn't reach their ends.
Inputs may be any that keep to these rules, and one draw needn't show every extreme that they name: `block_counts`: some sub-box holds exactly 3 blocks and some holds none, in every draw; slots at and past a sub-box's count hold no block. `block_coords`: the 3 columns of one sub-box name distinct blocks; row 0 is below 4, row 1 below 8, row 2 below 4.
All inputs are finite; a program needn't handle non-finite values. No bound on the sum of `fiber_mask` on one device may be relied on, other than what follows from the above.
Results may differ from the reference program's by a relative error of at most 0.0014.
Values may be sent and summed in bfloat16 or wider, within the bound.
A program may use at most 128 MiB of HBM per device.

```python
import jax
import jax.numpy as jnp
from jax import lax

R = 256
BLK = 128
SLOTS = 3
BX = 4
BY = 8
BZ = 4
SA = 512
SB = 1024
SC = 512
N_GX = 8
N_GY = 4
N_GZ = 8


def draw_block_counts(key, part):
    total = N_GX * N_GY * N_GZ
    first, second, third = jax.random.split(jax.random.fold_in(key, 11), 3)
    raw = jax.random.randint(first, (total,), 0, 5)
    table = jnp.array([0, 1, 1, 2, 3], jnp.int32)
    counts = jnp.minimum(table[raw], SLOTS)
    busiest = jax.random.randint(second, (), 0, total)
    emptiest = (busiest + 1 + jax.random.randint(third, (), 0, total - 1)) % total
    counts = counts.at[busiest].set(SLOTS).at[emptiest].set(0)
    return counts.reshape(N_GX, N_GY, N_GZ).astype(jnp.int32)


def draw_block_coords(key, part):
    total = N_GX * N_GY * N_GZ
    cells = BX * BY * BZ
    scores = jax.random.randint(jax.random.fold_in(key, 23), (total, cells), 0, 2 ** 30 // cells)
    scores = scores * cells + jnp.arange(cells, dtype=jnp.int32)[None, :]
    picks = jnp.argsort(-scores, axis=1)[:, :SLOTS].astype(jnp.int32)
    first = picks // (BY * BZ)
    second = picks // BZ % BY
    third = picks % BZ
    coords = jnp.stack([first, second, third], axis=1)
    return coords.reshape(N_GX, N_GY, N_GZ, 3, SLOTS).astype(jnp.int32)


def plant(values, rng, smallest, high):
    longest = values.shape.index(max(values.shape))
    spots = []
    for shift in (0, 1):
        where = [jax.random.randint(jax.random.fold_in(rng, axis), (), 0, length) for axis, length in enumerate(values.shape)]
        where[longest] = (where[longest] + shift) % values.shape[longest]
        spots.append(tuple(where))
    return values.at[spots[0]].set(smallest).at[spots[1]].set(high)


def levels(stream_key, dims, cuts, smallest, top_value):
    def one(position, shards_of):
        draws = jax.random.uniform(jax.random.fold_in(jax.random.fold_in(stream_key, 6), position), (shards_of,), jnp.float32, smallest / len(cuts), top_value / len(cuts))
        return jnp.repeat(jnp.exp(draws), dims[position] // shards_of).reshape((-1,) + (1,) * (len(dims) - position - 1))

    loudness = one(*cuts[0])
    for cut in cuts[1:]:
        loudness = loudness * one(*cut)
    return loudness


def setup_inputs(seed: int = 0) -> dict:
    streams_of = jax.random.split(jax.random.key(seed), 8)
    return {
        "tensor_blocks": jnp.clip(3.0 * jax.random.uniform(streams_of[0], (N_GX, N_GY, N_GZ, SLOTS, BLK, BLK, BLK), jnp.float32) ** levels(streams_of[0], (N_GX, N_GY, N_GZ, SLOTS, BLK, BLK, BLK), ((0, 8), (1, 4), (2, 8)), -0.2, 0.2), 0.0, 3.0).astype(jnp.bfloat16),
        "fiber_mask": plant((jax.random.randint(streams_of[1], (N_GX, N_GY, N_GZ, SLOTS, BLK, BLK), 0, 4) < 3).astype(jnp.int32), jax.random.fold_in(streams_of[1], 1), 0, 1),
        "block_coords": draw_block_coords(jax.random.fold_in(streams_of[7], 71), 0),
        "block_counts": draw_block_counts(jax.random.fold_in(streams_of[7], 71), 0),
        "factor_a": jnp.clip(jax.random.uniform(streams_of[4], (N_GX, SA, R), jnp.float32, -0.59765625, 0.59765625) * levels(streams_of[4], (N_GX, SA, R), ((0, 8), (1, 32)), -0.4, 0.0), -0.59765625, 0.59765625).astype(jnp.bfloat16),
        "factor_b": jnp.clip(jax.random.uniform(streams_of[5], (N_GY, SB, R), jnp.float32, -0.59765625, 0.59765625) * levels(streams_of[5], (N_GY, SB, R), ((0, 4), (1, 64)), -0.4, 0.0), -0.59765625, 0.59765625).astype(jnp.bfloat16),
        "factor_c": jnp.clip(jax.random.uniform(streams_of[6], (N_GZ, SC, R), jnp.float32, -0.59765625, 0.59765625) * levels(streams_of[6], (N_GZ, SC, R), ((0, 8), (1, 32)), -0.4, 0.0), -0.59765625, 0.59765625).astype(jnp.bfloat16),
    }


def block_terms(rows_a, rows_b, rows_c, entries, fibers):
    khatri = (rows_b[:, None, :].astype(jnp.float32) * rows_c[None, :, :].astype(jnp.float32)).astype(jnp.bfloat16)
    khatri = khatri.reshape(BLK * BLK, R)
    log_rate = jnp.dot(rows_a, khatri.T, preferred_element_type=jnp.float32)
    weight = fibers.astype(jnp.float32).reshape(BLK, BLK, 1)
    misfit = weight * (jnp.exp(log_rate.reshape(BLK, BLK, BLK)) - entries.astype(jnp.float32)) / BLK
    misfit = misfit.astype(jnp.bfloat16).reshape(BLK, BLK * BLK)
    part_a = jnp.dot(misfit, khatri, preferred_element_type=jnp.float32)
    folded = jnp.einsum("uk,ur->kr", misfit.astype(jnp.float32), rows_a.astype(jnp.float32))
    folded = folded.astype(jnp.bfloat16).reshape(BLK, BLK, R)
    part_b = jnp.einsum("vwr,wr->vr", folded.astype(jnp.float32), rows_c.astype(jnp.float32))
    part_c = jnp.einsum("vwr,vr->wr", folded.astype(jnp.float32), rows_b.astype(jnp.float32))
    return part_a, part_b, part_c


def add_rows(total, slab, start, part):
    anchor = jnp.zeros((), jnp.int32)
    current = lax.dynamic_slice(total, (slab.astype(jnp.int32), start.astype(jnp.int32), anchor), (1, BLK, R))
    return lax.dynamic_update_slice(total, current + part[None].astype(total.dtype),
                                    (slab.astype(jnp.int32), start.astype(jnp.int32), anchor))


def reference(tensor_blocks, fiber_mask, block_coords, block_counts, factor_a, factor_b, factor_c):
    def advance(totals, flat_index):
        flat_index = flat_index.astype(jnp.int32)
        device = (flat_index // SLOTS).astype(jnp.int32)
        slot_index = (flat_index % SLOTS).astype(jnp.int32)
        mode_one = (device // (N_GY * N_GZ)).astype(jnp.int32)
        mode_two = ((device // N_GZ) % N_GY).astype(jnp.int32)
        mode_three = (device % N_GZ).astype(jnp.int32)
        filled = block_counts[mode_one, mode_two, mode_three]

        def accumulate(totals):
            grad_a, grad_b, grad_c = totals
            anchor = jnp.zeros((), jnp.int32)
            coords = block_coords[mode_one, mode_two, mode_three]
            start_a = (coords[0, slot_index] * BLK).astype(jnp.int32)
            start_b = (coords[1, slot_index] * BLK).astype(jnp.int32)
            start_c = (coords[2, slot_index] * BLK).astype(jnp.int32)
            rows_a = lax.dynamic_slice(factor_a, (mode_one, start_a, anchor), (1, BLK, R))[0]
            rows_b = lax.dynamic_slice(factor_b, (mode_two, start_b, anchor), (1, BLK, R))[0]
            rows_c = lax.dynamic_slice(factor_c, (mode_three, start_c, anchor), (1, BLK, R))[0]
            entries = tensor_blocks[mode_one, mode_two, mode_three, slot_index]
            fibers = fiber_mask[mode_one, mode_two, mode_three, slot_index]
            part_a, part_b, part_c = block_terms(rows_a, rows_b, rows_c, entries, fibers)
            return (add_rows(grad_a, mode_one, start_a, part_a),
                    add_rows(grad_b, mode_two, start_b, part_b),
                    add_rows(grad_c, mode_three, start_c, part_c))

        return lax.cond(slot_index < filled, accumulate, lambda kept: kept, totals), None

    start = (jnp.zeros(factor_a.shape, jnp.float32), jnp.zeros(factor_b.shape, jnp.float32),
             jnp.zeros(factor_c.shape, jnp.float32))
    totals, _ = lax.scan(advance, start, jnp.arange(N_GX * N_GY * N_GZ * SLOTS, dtype=jnp.int32))
    return totals[0], totals[1], totals[2]
```

```python
import functools

import jax
import jax.numpy as jnp
from jax import lax
from jax.experimental import pallas as pl
from jax.experimental.pallas import tpu as pltpu
from jax.sharding import PartitionSpec as P

R = 256
BLK = 128
SLOTS = 3
SHARD = 16
NX, NY, NZ = 2, 4, 8
CHUNK = 16
F32 = jnp.float32
BF16 = jnp.bfloat16
MESH = pl.DeviceIdType.MESH
VMEM = pl.BlockSpec(memory_space=pltpu.VMEM)


class Place:
    def __init__(self):
        gx, gy, gz = lax.axis_index("gx"), lax.axis_index("gy"), lax.axis_index("gz")
        self.y, self.x_lo = gx // 2, gx % 2
        self.x_hi, self.core = gy // 2, gy % 2
        self.z = gz

    def at(self, y=None, x_lo=None, x_hi=None, core=None, z=None):
        y = self.y if y is None else y
        x_lo = self.x_lo if x_lo is None else x_lo
        x_hi = self.x_hi if x_hi is None else x_hi
        core = self.core if core is None else core
        z = self.z if z is None else z
        return (y * 2 + x_lo, x_hi * 2 + core, z)

    def greet(self):
        barrier = pltpu.get_barrier_semaphore()
        peers = [self.at(core=1 - self.core)]
        peers += [self.at(z=(self.z + k) % NZ) for k in range(1, NZ)]
        peers += [self.at(y=(self.y + k) % NY) for k in range(1, NY)]
        peers += [self.at(x_lo=lo, x_hi=hi) for lo, hi in self.x_peers()]
        for peer in peers:
            pl.semaphore_signal(barrier, inc=1, device_id=peer, device_id_type=MESH)
        pl.semaphore_wait(barrier, len(peers))

    def x_peers(self):
        lo, hi = self.x_lo, self.x_hi
        return [(1 - lo, hi), (lo, 1 - hi), (1 - lo, 1 - hi)]


class Copies:
    def __init__(self, send_sems, recv_sems):
        self.send_sems, self.recv_sems = send_sems, recv_sems
        self.n = 0
        self.started = []

    def start(self, src, dst, peer):
        copy = pltpu.make_async_remote_copy(
            src_ref=src,
            dst_ref=dst,
            send_sem=self.send_sems.at[self.n],
            recv_sem=self.recv_sems.at[self.n],
            device_id=peer,
            device_id_type=MESH,
        )
        self.n += 1
        copy.start()
        self.started.append(copy)
        return copy

    def drain(self):
        for copy in self.started:
            copy.wait_send()


def gather_kernel(fa, fb, fc, a, b, c, send_sems, recv_sems, own_sems):
    me = Place()
    copies = Copies(send_sems, recv_sems)
    block_a = me.x_hi * 2 + me.core
    block_b = me.y * 2 + me.x_lo
    block_c = (me.x_lo * 2 + me.x_hi) * 2 + me.core
    own = [
        pltpu.make_async_copy(fa.at[0], a.at[block_a, me.z], own_sems.at[0]),
        pltpu.make_async_copy(fb.at[0], b.at[block_b, me.z], own_sems.at[1]),
        pltpu.make_async_copy(fc.at[0], c.at[me.y, block_c], own_sems.at[2]),
    ]
    for copy in own:
        copy.start()
    me.greet()
    in_a, in_b, in_c = [], [], []
    for k in range(1, NZ):
        peer = me.at(z=(me.z + k) % NZ)
        in_b.append(copies.start(fb.at[0], b.at[block_b, me.z], peer))
        in_a.append(copies.start(fa.at[0], a.at[block_a, me.z], peer))
    for k in range(1, NY):
        peer = me.at(y=(me.y + k) % NY)
        in_c.append(copies.start(fc.at[0], c.at[me.y, block_c], peer))
    for copy in own:
        copy.wait()
    for copy in in_c:
        copy.wait_recv()
    part_c = c.at[:, block_c]
    in_c = [
        copies.start(part_c, part_c, me.at(x_lo=lo, x_hi=hi)) for lo, hi in me.x_peers()
    ]
    for copy in in_b:
        copy.wait_recv()
    in_b = [copies.start(b.at[block_b], b.at[block_b], me.at(x_lo=1 - me.x_lo))]
    for copy in in_a:
        copy.wait_recv()
    in_a = [copies.start(a.at[block_a], a.at[block_a], me.at(x_hi=1 - me.x_hi))]
    for copy in in_b:
        copy.wait_recv()
    part_b = b.at[pl.ds(me.y * 2, 2)]
    in_b = [
        copies.start(part_b, part_b, me.at(y=(me.y + k) % NY)) for k in range(1, NY)
    ]
    for copy in in_c:
        copy.wait_recv()
    other = me.at(core=1 - me.core)
    in_c = []
    for x in range(4):
        part_c = c.at[:, x * 2 + me.core]
        in_c.append(copies.start(part_c, part_c, other))
    for copy in in_a:
        copy.wait_recv()
    in_a = []
    for hi in range(2):
        part_a = a.at[hi * 2 + me.core]
        in_a.append(copies.start(part_a, part_a, other))
    for copy in in_a + in_b + in_c:
        copy.wait_recv()
    copies.drain()


def gather(fa, fb, fc):
    n = 7 + 7 + 3 + 3 + 1 + 1 + 3 + 4 + 2
    a, b, c = pl.pallas_call(
        gather_kernel,
        out_shape=(
            jax.ShapeDtypeStruct((4, NZ, SHARD, R), BF16),
            jax.ShapeDtypeStruct((8, NZ, SHARD, R), BF16),
            jax.ShapeDtypeStruct((4, 8, SHARD, R), BF16),
        ),
        in_specs=[VMEM] * 3,
        out_specs=(VMEM,) * 3,
        scratch_shapes=[
            pltpu.SemaphoreType.DMA((n,)),
            pltpu.SemaphoreType.DMA((n,)),
            pltpu.SemaphoreType.DMA((3,)),
        ],
        compiler_params=pltpu.CompilerParams(collective_id=0, has_side_effects=True),
        name="gather",
    )(fa, fb, fc)
    return a.reshape(512, R), b.reshape(1024, R), c.reshape(512, R)


def terms_kernel(
    coords, filled, x_ref, m_ref, a_ref, b_ref, c_ref, ga, gb, gc, xs, acc_a, acc_c, pb, cf
):
    slot, chunk = pl.program_id(0), pl.program_id(1)

    @pl.when((slot == 0) & (chunk == 0))
    def _():
        ga[...] = jnp.zeros_like(ga)
        gb[...] = jnp.zeros_like(gb)
        gc[...] = jnp.zeros_like(gc)

    @pl.when(slot < filled[0])
    def _():
        start_a = pl.multiple_of(coords[0, slot] * BLK, BLK)
        start_b = pl.multiple_of(coords[1, slot] * BLK, BLK)
        start_c = pl.multiple_of(coords[2, slot] * BLK, BLK)

        @pl.when(chunk == 0)
        def _():
            acc_a[...] = jnp.zeros_like(acc_a)
            acc_c[...] = jnp.zeros_like(acc_c)
            cf[...] = c_ref[pl.ds(start_c, BLK), :].astype(F32)

        for u in range(BLK):
            xs[pl.ds(u, CHUNK, stride=BLK), :] = x_ref[0, u].astype(F32)
        rows_a = a_ref[pl.ds(start_a, BLK), :]
        rows_c = c_ref[pl.ds(start_c, BLK), :]
        first_b = pl.multiple_of(start_b + chunk * CHUNK, CHUNK)
        rows_b = b_ref[pl.ds(first_b, CHUNK), :].astype(F32)
        scale = pltpu.roll(m_ref[0].astype(F32) * (1.0 / BLK), (BLK - chunk * CHUNK) % BLK, 1)
        for pair in range(CHUNK // 2):
            kh, mis = [], []
            for v in (2 * pair, 2 * pair + 1):
                row = jnp.broadcast_to(rows_b[v : v + 1, :], (16, R)).astype(BF16)
                kh.append((rows_c.reshape(8, 16, R) * row[None]).reshape(BLK, R))
            kh = jnp.concatenate(kh, 0)
            log_rate = lax.dot_general(
                rows_a, kh, (((1,), (1,)), ((), ())), preferred_element_type=F32
            )
            rate = jnp.exp(log_rate)
            for j, v in enumerate((2 * pair, 2 * pair + 1)):
                x = xs[v * BLK : (v + 1) * BLK, :]
                w = scale[:, v : v + 1]
                mis.append((w * (rate[:, j * BLK : (j + 1) * BLK] - x)).astype(BF16))
            mis = jnp.concatenate(mis, 1)
            acc_a[...] += jnp.dot(mis, kh, preferred_element_type=F32)
            folded = lax.dot_general(
                mis, rows_a, (((0,), (0,)), ((), ())), preferred_element_type=F32
            )
            folded = folded.astype(BF16).astype(F32)
            f0, f1 = folded[:BLK], folded[BLK:]
            pb[2 * pair] = (f0 * cf[...]).reshape(16, 8, R).sum(0)
            pb[2 * pair + 1] = (f1 * cf[...]).reshape(16, 8, R).sum(0)
            acc_c[...] += f0 * rows_b[2 * pair : 2 * pair + 1] + f1 * rows_b[2 * pair + 1 : 2 * pair + 2]
        gb[pl.ds(first_b, CHUNK), :] += pb[...].sum(1)

        @pl.when(chunk == BLK // CHUNK - 1)
        def _():
            ga[pl.ds(start_a, BLK), :] += acc_a[...]
            gc[pl.ds(start_c, BLK), :] += acc_c[...]


def terms(blocks, fibers, coords, filled, a, b, c):
    last = BLK // CHUNK - 1

    def held(slot, filled):
        return jnp.minimum(slot, jnp.maximum(filled[0] - 1, 0))

    def x_block(slot, chunk, coords, filled):
        return (held(slot, filled), 0, jnp.where(slot < filled[0], chunk, last), 0)

    def m_block(slot, chunk, coords, filled):
        return (held(slot, filled), 0, 0)

    def whole(slot, chunk, coords, filled):
        return (0, 0)

    return pl.pallas_call(
        terms_kernel,
        out_shape=(
            jax.ShapeDtypeStruct((512, R), F32),
            jax.ShapeDtypeStruct((1024, R), F32),
            jax.ShapeDtypeStruct((512, R), F32),
        ),
        grid_spec=pltpu.PrefetchScalarGridSpec(
            num_scalar_prefetch=2,
            grid=(SLOTS, BLK // CHUNK),
            in_specs=[
                pl.BlockSpec((1, BLK, CHUNK, BLK), x_block),
                pl.BlockSpec((1, BLK, BLK), m_block),
                pl.BlockSpec((512, R), whole),
                pl.BlockSpec((1024, R), whole),
                pl.BlockSpec((512, R), whole),
            ],
            out_specs=(
                pl.BlockSpec((512, R), whole),
                pl.BlockSpec((1024, R), whole),
                pl.BlockSpec((512, R), whole),
            ),
            scratch_shapes=[
                pltpu.VMEM((CHUNK * BLK, BLK), F32),
                pltpu.VMEM((BLK, R), F32),
                pltpu.VMEM((BLK, R), F32),
                pltpu.VMEM((CHUNK, 8, R), F32),
                pltpu.VMEM((BLK, R), F32),
            ],
        ),
        name="terms",
    )(coords, filled, blocks, fibers, a, b, c)


def scatter_kernel(
    ga, gb, gc, out_a, out_b, out_c,
    a1, a2, a3, sa1, sa2, b1, b2, b3, d1, d2, d3, sb1, sb2, sd1, sd2, c1, c2, c3, sc1, sc2,
    send_sems, recv_sems,
):
    me = Place()
    copies = Copies(send_sems, recv_sems)
    me.greet()
    other = me.at(core=1 - me.core)
    left, right = slice(0, 128), slice(128, 256)
    in_b, in_d = [], []
    for k in range(1, NY):
        there = (me.y + k) % NY
        in_b.append(copies.start(gb.at[there, :, :, :, left], b1.at[k - 1], me.at(y=there)))
    to = 1 - me.x_lo
    for y in range(NY):
        in_d.append(copies.start(gb.at[y, to, :, :, right], d1.at[y], me.at(x_lo=to)))
    in_a = [
        copies.start(ga.at[hi, 1 - me.core], a1.at[hi], other) for hi in range(2)
    ]
    in_c = [copies.start(gc.at[:, 1 - me.core], c1, other)]
    for copy in in_a:
        copy.wait_recv()
    for hi in range(2):
        sa1[hi] = ga[hi, me.core] + a1[hi]
    in_a = [copies.start(sa1.at[1 - me.x_hi], a2, me.at(x_hi=1 - me.x_hi))]
    for copy in in_c:
        copy.wait_recv()
    sc1[...] = gc[:, me.core] + c1[...]
    in_c = []
    for k in range(1, NY):
        there = (me.y + k) % NY
        in_c.append(copies.start(sc1.at[pl.ds(there * 4, 4)], c2.at[k - 1], me.at(y=there)))
    for copy in in_d:
        copy.wait_recv()
    for y in range(NY):
        sd1[y] = gb[y, me.x_lo, :, :, right] + d1[y]
    in_d = []
    for k in range(1, NY):
        there = (me.y + k) % NY
        in_d.append(copies.start(sd1.at[there], d2.at[k - 1], me.at(y=there)))
    for copy in in_b:
        copy.wait_recv()
    sb1[...] = gb[me.y, :, :, :, left] + b1[0] + b1[1] + b1[2]
    in_b = [copies.start(sb1.at[to], b2, me.at(x_lo=to))]
    for copy in in_a:
        copy.wait_recv()
    sa2[...] = sa1[me.x_hi] + a2[...]
    in_a = []
    for k in range(1, NZ):
        there = (me.z + k) % NZ
        in_a.append(copies.start(sa2.at[there], a3.at[k - 1], me.at(z=there)))
    for copy in in_c:
        copy.wait_recv()
    sc2[...] = sc1[pl.ds(me.y * 4, 4)] + c2[0] + c2[1] + c2[2]
    in_c = []
    for k, (lo, hi) in enumerate(me.x_peers()):
        in_c.append(copies.start(sc2.at[lo * 2 + hi], c3.at[k], me.at(x_lo=lo, x_hi=hi)))
    for copy in in_d:
        copy.wait_recv()
    sd2[...] = sd1[me.y] + d2[0] + d2[1] + d2[2]
    in_d = []
    for k in range(1, NZ):
        there = (me.z + k) % NZ
        in_d.append(copies.start(sd2.at[there], d3.at[k - 1], me.at(z=there)))
    for copy in in_b:
        copy.wait_recv()
    sb2[...] = sb1[me.x_lo] + b2[...]
    in_b = []
    for k in range(1, NZ):
        there = (me.z + k) % NZ
        in_b.append(copies.start(sb2.at[there], b3.at[k - 1], me.at(z=there)))
    for copy in in_c:
        copy.wait_recv()
    out_c[0] = sc2[me.x_lo * 2 + me.x_hi] + c3[0] + c3[1] + c3[2]
    for copy in in_a:
        copy.wait_recv()
    out_a[0] = sa2[me.z] + a3[...].sum(0)
    for copy in in_d:
        copy.wait_recv()
    out_b[0, :, right] = sd2[me.z] + d3[...].sum(0)
    for copy in in_b:
        copy.wait_recv()
    out_b[0, :, left] = sb2[me.z] + b3[...].sum(0)
    copies.drain()


def scatter(ga, gb, gc):
    n = 3 + 4 + 2 + 1 + 1 + 3 + 3 + 1 + 7 + 3 + 7 + 7
    half = R // 2

    def buf(*shape):
        return pltpu.VMEM(shape, F32)

    return pl.pallas_call(
        scatter_kernel,
        out_shape=(jax.ShapeDtypeStruct((1, SHARD, R), F32),) * 3,
        in_specs=[VMEM] * 3,
        out_specs=(VMEM,) * 3,
        scratch_shapes=[
            buf(2, NZ, SHARD, R), buf(NZ, SHARD, R), buf(7, SHARD, R),
            buf(2, NZ, SHARD, R), buf(NZ, SHARD, R),
            buf(3, 2, NZ, SHARD, half), buf(NZ, SHARD, half), buf(7, SHARD, half),
            buf(4, NZ, SHARD, half), buf(3, NZ, SHARD, half), buf(7, SHARD, half),
            buf(2, NZ, SHARD, half), buf(NZ, SHARD, half),
            buf(4, NZ, SHARD, half), buf(NZ, SHARD, half),
            buf(16, SHARD, R), buf(3, 4, SHARD, R), buf(3, SHARD, R),
            buf(16, SHARD, R), buf(4, SHARD, R),
            pltpu.SemaphoreType.DMA((n,)),
            pltpu.SemaphoreType.DMA((n,)),
        ],
        compiler_params=pltpu.CompilerParams(collective_id=1, has_side_effects=True),
        name="scatter",
    )(
        ga.reshape(2, 2, NZ, SHARD, R),
        gb.reshape(NY, 2, NZ, SHARD, R),
        gc.reshape(16, 2, SHARD, R),
    )


def per_device(tensor_blocks, fiber_mask, block_coords, block_counts, factor_a, factor_b, factor_c):
    a, b, c = gather(factor_a, factor_b, factor_c)
    ga, gb, gc = terms(
        tensor_blocks.reshape(SLOTS, BLK, BLK, BLK),
        fiber_mask.reshape(SLOTS, BLK, BLK),
        block_coords.reshape(3, SLOTS),
        block_counts.reshape(1),
        a, b, c,
    )
    return scatter(ga, gb, gc)


def solution(mesh):
    placed = (
        P("gx", "gy", "gz", None, None, None, None),
        P("gx", "gy", "gz", None, None, None),
        P("gx", "gy", "gz", None, None),
        P("gx", "gy", "gz"),
        P("gx", ("gy", "gz"), None),
        P("gy", ("gx", "gz"), None),
        P("gz", ("gx", "gy"), None),
    )
    return jax.shard_map(
        per_device,
        mesh=mesh,
        in_specs=placed,
        out_specs=(
            P("gx", ("gy", "gz"), None),
            P("gy", ("gx", "gz"), None),
            P("gz", ("gx", "gy"), None),
        ),
        check_vma=False,
    )
```

```python
import functools

import jax
import jax.numpy as jnp
from jax import lax
from jax.experimental import pallas as pl
from jax.experimental.pallas import tpu as pltpu
from jax.sharding import PartitionSpec as P

R = 256
BLK = 128
SLOTS = 3
SHARD = 16
NX, NY, NZ = 2, 4, 8
CHUNK = 16
F32 = jnp.float32
BF16 = jnp.bfloat16
MESH = pl.DeviceIdType.MESH
VMEM = pl.BlockSpec(memory_space=pltpu.VMEM)


class Place:
    def __init__(self):
        gx, gy, gz = lax.axis_index("gx"), lax.axis_index("gy"), lax.axis_index("gz")
        self.y, self.x_lo = gx // 2, gx % 2
        self.x_hi, self.core = gy // 2, gy % 2
        self.z = gz

    def at(self, y=None, x_lo=None, x_hi=None, core=None, z=None):
        y = self.y if y is None else y
        x_lo = self.x_lo if x_lo is None else x_lo
        x_hi = self.x_hi if x_hi is None else x_hi
        core = self.core if core is None else core
        z = self.z if z is None else z
        return (y * 2 + x_lo, x_hi * 2 + core, z)

    def greet(self):
        barrier = pltpu.get_barrier_semaphore()
        peers = [self.at(core=1 - self.core)]
        peers += [self.at(z=(self.z + k) % NZ) for k in range(1, NZ)]
        peers += [self.at(y=(self.y + k) % NY) for k in range(1, NY)]
        peers += [self.at(x_lo=lo, x_hi=hi) for lo, hi in self.x_peers()]
        for peer in peers:
            pl.semaphore_signal(barrier, inc=1, device_id=peer, device_id_type=MESH)
        pl.semaphore_wait(barrier, len(peers))

    def x_peers(self):
        lo, hi = self.x_lo, self.x_hi
        return [(1 - lo, hi), (lo, 1 - hi), (1 - lo, 1 - hi)]


class Copies:
    def __init__(self, send_sems, recv_sems):
        self.send_sems, self.recv_sems = send_sems, recv_sems
        self.n = 0
        self.started = []

    def start(self, src, dst, peer):
        copy = pltpu.make_async_remote_copy(
            src_ref=src,
            dst_ref=dst,
            send_sem=self.send_sems.at[self.n],
            recv_sem=self.recv_sems.at[self.n],
            device_id=peer,
            device_id_type=MESH,
        )
        self.n += 1
        copy.start()
        self.started.append(copy)
        return copy

    def drain(self):
        for copy in self.started:
            copy.wait_send()


def gather_kernel(fa, fb, fc, a, b, c, send_sems, recv_sems, own_sems):
    me = Place()
    copies = Copies(send_sems, recv_sems)
    block_a = me.x_hi * 2 + me.core
    block_b = me.y * 2 + me.x_lo
    block_c = (me.x_lo * 2 + me.x_hi) * 2 + me.core
    own = [
        pltpu.make_async_copy(fa.at[0], a.at[block_a, me.z], own_sems.at[0]),
        pltpu.make_async_copy(fb.at[0], b.at[block_b, me.z], own_sems.at[1]),
        pltpu.make_async_copy(fc.at[0], c.at[me.y, block_c], own_sems.at[2]),
    ]
    for copy in own:
        copy.start()
    me.greet()
    in_a, in_b, in_c = [], [], []
    for k in range(1, NZ):
        peer = me.at(z=(me.z + k) % NZ)
        in_b.append(copies.start(fb.at[0], b.at[block_b, me.z], peer))
        in_a.append(copies.start(fa.at[0], a.at[block_a, me.z], peer))
    for k in range(1, NY):
        peer = me.at(y=(me.y + k) % NY)
        in_c.append(copies.start(fc.at[0], c.at[me.y, block_c], peer))
    for copy in own:
        copy.wait()
    for copy in in_c:
        copy.wait_recv()
    part_c = c.at[:, block_c]
    in_c = [
        copies.start(part_c, part_c, me.at(x_lo=lo, x_hi=hi)) for lo, hi in me.x_peers()
    ]
    for copy in in_b:
        copy.wait_recv()
    in_b = [copies.start(b.at[block_b], b.at[block_b], me.at(x_lo=1 - me.x_lo))]
    for copy in in_a:
        copy.wait_recv()
    in_a = [copies.start(a.at[block_a], a.at[block_a], me.at(x_hi=1 - me.x_hi))]
    for copy in in_b:
        copy.wait_recv()
    part_b = b.at[pl.ds(me.y * 2, 2)]
    in_b = [
        copies.start(part_b, part_b, me.at(y=(me.y + k) % NY)) for k in range(1, NY)
    ]
    for copy in in_c:
        copy.wait_recv()
    other = me.at(core=1 - me.core)
    in_c = []
    for x in range(4):
        part_c = c.at[:, x * 2 + me.core]
        in_c.append(copies.start(part_c, part_c, other))
    for copy in in_a:
        copy.wait_recv()
    in_a = []
    for hi in range(2):
        part_a = a.at[hi * 2 + me.core]
        in_a.append(copies.start(part_a, part_a, other))
    for copy in in_a + in_b + in_c:
        copy.wait_recv()
    copies.drain()


def gather(fa, fb, fc):
    n = 7 + 7 + 3 + 3 + 1 + 1 + 3 + 4 + 2
    a, b, c = pl.pallas_call(
        gather_kernel,
        out_shape=(
            jax.ShapeDtypeStruct((4, NZ, SHARD, R), BF16),
            jax.ShapeDtypeStruct((8, NZ, SHARD, R), BF16),
            jax.ShapeDtypeStruct((4, 8, SHARD, R), BF16),
        ),
        in_specs=[VMEM] * 3,
        out_specs=(VMEM,) * 3,
        scratch_shapes=[
            pltpu.SemaphoreType.DMA((n,)),
            pltpu.SemaphoreType.DMA((n,)),
            pltpu.SemaphoreType.DMA((3,)),
        ],
        compiler_params=pltpu.CompilerParams(collective_id=0, has_side_effects=True),
        name="gather",
    )(fa, fb, fc)
    return a.reshape(512, R), b.reshape(1024, R), c.reshape(512, R)


def terms_kernel(
    coords, filled, x_ref, m_ref, a_ref, b_ref, c_ref, ga, gb, gc, xs, acc_a, acc_c, pb, cf, perm, kh_s, mis_s
):
    slot, chunk = pl.program_id(0), pl.program_id(1)

    @pl.when((slot == 0) & (chunk == 0))
    def _():
        ga[...] = jnp.zeros_like(ga)
        gb[...] = jnp.zeros_like(gb)
        gc[...] = jnp.zeros_like(gc)
        row = lax.broadcasted_iota(jnp.int32, (256, 256), 0)
        col = lax.broadcasted_iota(jnp.int32, (256, 256), 1)
        swapped = (row % 16) * 16 + row // 16
        perm[...] = jnp.where(col == swapped, 1.0, 0.0).astype(BF16)

    @pl.when(slot < filled[0])
    def _():
        start_a = pl.multiple_of(coords[0, 0, slot] * BLK, BLK)
        start_b = pl.multiple_of(coords[1, 0, slot] * BLK, BLK)
        start_c = pl.multiple_of(coords[2, 0, slot] * BLK, BLK)

        @pl.when(chunk == 0)
        def _():
            acc_a[...] = jnp.zeros_like(acc_a)
            acc_c[...] = jnp.zeros_like(acc_c)
            cf[...] = c_ref[pl.ds(start_c, BLK), :].astype(F32)

        for g in range(BLK // 16):
            xg = x_ref[0, 16 * g : 16 * g + 16].reshape(256, BLK)
            xg = jnp.dot(perm[...], xg, preferred_element_type=F32)
            xs[:, 16 * g : 16 * g + 16, :] = xg.reshape(16, 16, BLK)
        rows_a = a_ref[pl.ds(start_a, BLK), :]
        rows_c = c_ref[pl.ds(start_c, BLK), :]
        first_b = pl.multiple_of(start_b + chunk * CHUNK, CHUNK)
        rows_b = b_ref[pl.ds(first_b, CHUNK), :].astype(F32)
        scale = pltpu.roll(m_ref[0].astype(F32) * (1.0 / BLK), (BLK - chunk * CHUNK) % BLK, 1)
        for pair in range(CHUNK // 2):
            kh, mis = [], []
            for v in (2 * pair, 2 * pair + 1):
                row = jnp.broadcast_to(rows_b[v : v + 1, :], (16, R)).astype(BF16)
                kh.append((rows_c.reshape(8, 16, R) * row[None]).reshape(BLK, R))
            kh = jnp.concatenate(kh, 0)
            kh_s[256 * pair : 256 * pair + 256, :] = kh
            log_rate = lax.dot_general(
                rows_a, kh, (((1,), (1,)), ((), ())), preferred_element_type=F32
            )
            rate = jnp.exp(log_rate)
            for j, v in enumerate((2 * pair, 2 * pair + 1)):
                x = xs[v]
                w = scale[:, v : v + 1]
                mis.append((w * (rate[:, j * BLK : (j + 1) * BLK] - x)).astype(BF16))
            mis = jnp.concatenate(mis, 1)
            mis_s[:, 256 * pair : 256 * pair + 256] = mis
            folded = lax.dot_general(
                mis, rows_a, (((0,), (0,)), ((), ())), preferred_element_type=F32
            )
            folded = folded.astype(BF16).astype(F32)
            f0, f1 = folded[:BLK], folded[BLK:]
            pb[2 * pair] = (f0 * cf[...]).reshape(16, 8, R).sum(0)
            pb[2 * pair + 1] = (f1 * cf[...]).reshape(16, 8, R).sum(0)
            acc_c[...] += f0 * rows_b[2 * pair : 2 * pair + 1] + f1 * rows_b[2 * pair + 1 : 2 * pair + 2]
        acc_a[...] += jnp.dot(mis_s[...], kh_s[...], preferred_element_type=F32)
        gb[pl.ds(first_b, CHUNK), :] += pb[...].sum(1)

        @pl.when(chunk == BLK // CHUNK - 1)
        def _():
            ga[pl.ds(start_a, BLK), :] += acc_a[...]
            gc[pl.ds(start_c, BLK), :] += acc_c[...]


def terms(blocks, fibers, coords, filled, a, b, c):
    last = BLK // CHUNK - 1

    def held(slot, filled):
        return jnp.minimum(slot, jnp.maximum(filled[0] - 1, 0))

    def x_block(slot, chunk, coords, filled):
        return (held(slot, filled), 0, jnp.where(slot < filled[0], chunk, last), 0)

    def m_block(slot, chunk, coords, filled):
        return (held(slot, filled), 0, 0)

    def whole(slot, chunk, coords, filled):
        return (0, 0)

    return pl.pallas_call(
        terms_kernel,
        out_shape=(
            jax.ShapeDtypeStruct((512, R), F32),
            jax.ShapeDtypeStruct((1024, R), F32),
            jax.ShapeDtypeStruct((512, R), F32),
        ),
        grid_spec=pltpu.PrefetchScalarGridSpec(
            num_scalar_prefetch=2,
            grid=(SLOTS, BLK // CHUNK),
            in_specs=[
                pl.BlockSpec((1, BLK, CHUNK, BLK), x_block),
                pl.BlockSpec((1, BLK, BLK), m_block),
                pl.BlockSpec((512, R), whole),
                pl.BlockSpec((1024, R), whole),
                pl.BlockSpec((512, R), whole),
            ],
            out_specs=(
                pl.BlockSpec((512, R), whole),
                pl.BlockSpec((1024, R), whole),
                pl.BlockSpec((512, R), whole),
            ),
            scratch_shapes=[
                pltpu.VMEM((CHUNK, BLK, BLK), F32),
                pltpu.VMEM((BLK, R), F32),
                pltpu.VMEM((BLK, R), F32),
                pltpu.VMEM((CHUNK, 8, R), F32),
                pltpu.VMEM((BLK, R), F32),
                pltpu.VMEM((256, 256), BF16),
                pltpu.VMEM((CHUNK * BLK, R), BF16),
                pltpu.VMEM((BLK, CHUNK * BLK), BF16),
            ],
        ),
        name="terms",
    )(coords, filled, blocks, fibers, a, b, c)


def scatter_kernel(
    ga, gb, gc, out,
    a1, a2, a3, sa1, sa2, b1, b2, b3, d1, d2, d3, sb1, sb2, sd1, sd2, c1, c2, c3, sc1, sc2,
    send_sems, recv_sems,
):
    me = Place()
    copies = Copies(send_sems, recv_sems)
    me.greet()
    other = me.at(core=1 - me.core)
    left, right = slice(0, 128), slice(128, 256)
    in_b, in_d = [], []
    for k in range(1, NY):
        there = (me.y + k) % NY
        in_b.append(copies.start(gb.at[there, :, :, :, left], b1.at[k - 1], me.at(y=there)))
    to = 1 - me.x_lo
    for y in range(NY):
        in_d.append(copies.start(gb.at[y, to, :, :, right], d1.at[y], me.at(x_lo=to)))
    in_a = [
        copies.start(ga.at[hi, 1 - me.core], a1.at[hi], other) for hi in range(2)
    ]
    in_c = [copies.start(gc.at[:, 1 - me.core], c1, other)]
    for copy in in_a:
        copy.wait_recv()
    for hi in range(2):
        sa1[hi] = ga[hi, me.core] + a1[hi]
    in_a = [copies.start(sa1.at[1 - me.x_hi], a2, me.at(x_hi=1 - me.x_hi))]
    for copy in in_c:
        copy.wait_recv()
    sc1[...] = gc[:, me.core] + c1[...]
    in_c = []
    for k in range(1, NY):
        there = (me.y + k) % NY
        in_c.append(copies.start(sc1.at[pl.ds(there * 4, 4)], c2.at[k - 1], me.at(y=there)))
    for copy in in_d:
        copy.wait_recv()
    for y in range(NY):
        sd1[y] = gb[y, me.x_lo, :, :, right] + d1[y]
    in_d = []
    for k in range(1, NY):
        there = (me.y + k) % NY
        in_d.append(copies.start(sd1.at[there], d2.at[k - 1], me.at(y=there)))
    for copy in in_b:
        copy.wait_recv()
    sb1[...] = gb[me.y, :, :, :, left] + b1[0] + b1[1] + b1[2]
    in_b = [copies.start(sb1.at[to], b2, me.at(x_lo=to))]
    for copy in in_a:
        copy.wait_recv()
    sa2[...] = sa1[me.x_hi] + a2[...]
    in_a = []
    for k in range(1, NZ):
        there = (me.z + k) % NZ
        in_a.append(copies.start(sa2.at[there], a3.at[k - 1], me.at(z=there)))
    for copy in in_c:
        copy.wait_recv()
    sc2[...] = sc1[pl.ds(me.y * 4, 4)] + c2[0] + c2[1] + c2[2]
    in_c = []
    for k, (lo, hi) in enumerate(me.x_peers()):
        in_c.append(copies.start(sc2.at[lo * 2 + hi], c3.at[k], me.at(x_lo=lo, x_hi=hi)))
    for copy in in_d:
        copy.wait_recv()
    sd2[...] = sd1[me.y] + d2[0] + d2[1] + d2[2]
    in_d = []
    for k in range(1, NZ):
        there = (me.z + k) % NZ
        in_d.append(copies.start(sd2.at[there], d3.at[k - 1], me.at(z=there)))
    for copy in in_b:
        copy.wait_recv()
    sb2[...] = sb1[me.x_lo] + b2[...]
    in_b = []
    for k in range(1, NZ):
        there = (me.z + k) % NZ
        in_b.append(copies.start(sb2.at[there], b3.at[k - 1], me.at(z=there)))
    for copy in in_c:
        copy.wait_recv()
    out[2] = sc2[me.x_lo * 2 + me.x_hi] + c3[0] + c3[1] + c3[2]
    for copy in in_a:
        copy.wait_recv()
    out[0] = sa2[me.z] + a3[...].sum(0)
    for copy in in_d:
        copy.wait_recv()
    out[1, :, right] = sd2[me.z] + d3[...].sum(0)
    for copy in in_b:
        copy.wait_recv()
    out[1, :, left] = sb2[me.z] + b3[...].sum(0)
    copies.drain()


def scatter(ga, gb, gc):
    n = 3 + 4 + 2 + 1 + 1 + 3 + 3 + 1 + 7 + 3 + 7 + 7
    half = R // 2

    def buf(*shape):
        return pltpu.VMEM(shape, F32)

    out = pl.pallas_call(
        scatter_kernel,
        out_shape=jax.ShapeDtypeStruct((3, SHARD, R), F32),
        in_specs=[VMEM] * 3,
        out_specs=VMEM,
        scratch_shapes=[
            buf(2, NZ, SHARD, R), buf(NZ, SHARD, R), buf(7, SHARD, R),
            buf(2, NZ, SHARD, R), buf(NZ, SHARD, R),
            buf(3, 2, NZ, SHARD, half), buf(NZ, SHARD, half), buf(7, SHARD, half),
            buf(4, NZ, SHARD, half), buf(3, NZ, SHARD, half), buf(7, SHARD, half),
            buf(2, NZ, SHARD, half), buf(NZ, SHARD, half),
            buf(4, NZ, SHARD, half), buf(NZ, SHARD, half),
            buf(16, SHARD, R), buf(3, 4, SHARD, R), buf(3, SHARD, R),
            buf(16, SHARD, R), buf(4, SHARD, R),
            pltpu.SemaphoreType.DMA((n,)),
            pltpu.SemaphoreType.DMA((n,)),
        ],
        compiler_params=pltpu.CompilerParams(collective_id=1, has_side_effects=True),
        name="scatter",
    )(
        ga.reshape(2, 2, NZ, SHARD, R),
        gb.reshape(NY, 2, NZ, SHARD, R),
        gc.reshape(16, 2, SHARD, R),
    )
    return pl.pallas_call(
        part_kernel,
        out_shape=(jax.ShapeDtypeStruct((1, SHARD, R), F32),) * 3,
        in_specs=[VMEM],
        out_specs=(VMEM,) * 3,
        name="part",
    )(out)


def part_kernel(rows, a, b, c):
    for i, ref in enumerate((a, b, c)):
        ref[0] = rows[i]


def per_device(tensor_blocks, fiber_mask, block_coords, block_counts, factor_a, factor_b, factor_c):
    a, b, c = gather(factor_a, factor_b, factor_c)
    ga, gb, gc = terms(
        tensor_blocks.reshape(SLOTS, BLK, BLK, BLK),
        fiber_mask.reshape(SLOTS, BLK, BLK),
        block_coords.reshape(3, 1, SLOTS),
        block_counts.reshape(1),
        a, b, c,
    )
    return scatter(ga, gb, gc)


def solution(mesh):
    placed = (
        P("gx", "gy", "gz", None, None, None, None),
        P("gx", "gy", "gz", None, None, None),
        P("gx", "gy", "gz", None, None),
        P("gx", "gy", "gz"),
        P("gx", ("gy", "gz"), None),
        P("gy", ("gx", "gz"), None),
        P("gz", ("gx", "gy"), None),
    )
    return jax.shard_map(
        per_device,
        mesh=mesh,
        in_specs=placed,
        out_specs=(
            P("gx", ("gy", "gz"), None),
            P("gy", ("gx", "gz"), None),
            P("gz", ("gx", "gy"), None),
        ),
        check_vma=False,
    )
```

```python
import functools

import jax
import jax.numpy as jnp
from jax import lax
from jax.experimental import pallas as pl
from jax.experimental.pallas import tpu as pltpu
from jax.sharding import PartitionSpec as P

R = 256
BLK = 128
SLOTS = 3
SHARD = 16
NX, NY, NZ = 2, 4, 8
CHUNK = 16
CHUNKS = BLK // CHUNK
NV = 8
UNIT = 8
F32 = jnp.float32
BF16 = jnp.bfloat16
MESH = pl.DeviceIdType.MESH
VMEM = pl.BlockSpec(memory_space=pltpu.VMEM)


class Place:
    def __init__(self):
        gx, gy, gz = lax.axis_index("gx"), lax.axis_index("gy"), lax.axis_index("gz")
        self.y, self.x_lo = gx // 2, gx % 2
        self.x_hi, self.core = gy // 2, gy % 2
        self.z = gz

    def at(self, y=None, x_lo=None, x_hi=None, core=None, z=None):
        y = self.y if y is None else y
        x_lo = self.x_lo if x_lo is None else x_lo
        x_hi = self.x_hi if x_hi is None else x_hi
        core = self.core if core is None else core
        z = self.z if z is None else z
        return (y * 2 + x_lo, x_hi * 2 + core, z)

    def greet(self):
        barrier = pltpu.get_barrier_semaphore()
        peers = [self.at(core=1 - self.core)]
        peers += [self.at(z=(self.z + k) % NZ) for k in range(1, NZ)]
        peers += [self.at(y=(self.y + k) % NY) for k in range(1, NY)]
        peers += [self.at(x_lo=lo, x_hi=hi) for lo, hi in self.x_peers()]
        for peer in peers:
            pl.semaphore_signal(barrier, inc=1, device_id=peer, device_id_type=MESH)
        self.greeted = len(peers)

    def met(self):
        pl.semaphore_wait(pltpu.get_barrier_semaphore(), self.greeted)

    def x_peers(self):
        lo, hi = self.x_lo, self.x_hi
        return [(1 - lo, hi), (lo, 1 - hi), (1 - lo, 1 - hi)]


class Copies:
    def __init__(self, send_sems, recv_sems):
        self.send_sems, self.recv_sems = send_sems, recv_sems
        self.n = 0
        self.started = []

    def start(self, src, dst, peer):
        copy = pltpu.make_async_remote_copy(
            src_ref=src,
            dst_ref=dst,
            send_sem=self.send_sems.at[self.n],
            recv_sem=self.recv_sems.at[self.n],
            device_id=peer,
            device_id_type=MESH,
        )
        self.n += 1
        copy.start()
        self.started.append(copy)
        return copy

    def drain(self):
        for copy in self.started:
            copy.wait_send()


def turn_chunks(lo, hi, x, xt, xin, xout, perm, in_sems, out_sems):
    def source(i):
        return x.at[i // CHUNKS, :, pl.ds(pl.multiple_of(i % CHUNKS * CHUNK, CHUNK), CHUNK), :]

    def load(i):
        return pltpu.make_async_copy(source(i), xin.at[i % 2], in_sems.at[i % 2])

    def store(i):
        return pltpu.make_async_copy(xout.at[i % 2], xt.at[i], out_sems.at[i % 2])

    if lo == 0:
        load(0).start()

    def body(i, carry):
        load(i).wait()

        @pl.when(i < SLOTS * CHUNKS - 1)
        def _():
            load(i + 1).start()

        @pl.when(i >= 2)
        def _():
            store(i - 2).wait()

        for g in range(BLK // UNIT):
            us = slice(UNIT * g, UNIT * g + UNIT)
            rows = xin[i % 2, us].reshape(UNIT * CHUNK, BLK)
            rows = jnp.dot(perm[...], rows, preferred_element_type=F32).astype(BF16)
            xout[i % 2, :, us, :] = rows.reshape(CHUNK, UNIT, BLK)
        store(i).start()
        return carry

    lax.fori_loop(lo, hi, body, 0)
    if hi == SLOTS * CHUNKS:
        store(hi - 2).wait()
        store(hi - 1).wait()


NEAR = (0, 7, 1, 6, 2, 5, 3, 4)


def gather_kernel(
    fa, fb, fc, x, a, b, c, xt, xin, xout, perm, send_sems, recv_sems, own_sems, in_sems, out_sems
):
    me = Place()
    copies = Copies(send_sems, recv_sems)
    turn = functools.partial(
        turn_chunks, x=x, xt=xt, xin=xin, xout=xout, perm=perm, in_sems=in_sems, out_sems=out_sems
    )
    block_a = me.x_hi * 2 + me.core
    block_b = me.y * 2 + me.x_lo
    block_c = (me.x_lo * 2 + me.x_hi) * 2 + me.core
    me.greet()
    own = [
        pltpu.make_async_copy(fb.at[0], b.at[block_b, me.z], own_sems.at[0]),
        pltpu.make_async_copy(fa.at[0], a.at[block_a, me.z], own_sems.at[1]),
        pltpu.make_async_copy(fc.at[0], c.at[me.y, block_c], own_sems.at[2]),
    ]
    for copy in own:
        copy.start()
    row = lax.broadcasted_iota(jnp.int32, perm.shape, 0)
    col = lax.broadcasted_iota(jnp.int32, perm.shape, 1)
    swapped = (row % UNIT) * CHUNK + row // UNIT
    perm[...] = jnp.where(col == swapped, 1.0, 0.0).astype(BF16)
    turn(0, 4)
    me.met()
    z_b, z_a, y_c = {}, {}, []
    for k in reversed(NEAR[1:]):
        z_b[k] = copies.start(fb.at[0], b.at[block_b, me.z], me.at(z=(me.z + k) % NZ))
    for k in range(1, NY):
        y_c.append(copies.start(fc.at[0], c.at[me.y, block_c], me.at(y=(me.y + k) % NY)))
    for k in reversed(NEAR[1:]):
        z_a[k] = copies.start(fa.at[0], a.at[block_a, me.z], me.at(z=(me.z + k) % NZ))
    up, down = me.at(y=(me.y + 1) % NY), me.at(y=(me.y + NY - 1) % NY)
    above, below = (me.y + 1) % NY, (me.y + NY - 1) % NY
    beside = me.at(x_lo=1 - me.x_lo)

    def piece(y, x_lo, k):
        return b.at[y * 2 + x_lo, (me.z + NZ - k) % NZ]

    def send(ref, peer):
        return copies.start(ref, ref, peer)

    for copy in own:
        copy.wait()
    to_x, to_up, to_down = {}, {}, {}

    def spread(k):
        if k:
            z_b[k].wait_recv()
        ref = piece(me.y, me.x_lo, k)
        to_x[k] = send(ref, beside)
        to_up[0, k] = send(ref, up)
        to_down[0, k] = send(ref, down)

    spread(0)
    turn(4, 10)
    for k in NEAR[1:]:
        spread(k)
    for copy in y_c:
        copy.wait_recv()
    part_c = c.at[:, block_c]
    x_c = [send(part_c, me.at(x_lo=lo, x_hi=hi)) for lo, hi in me.x_peers()]
    other = me.at(core=1 - me.core)
    for k in NEAR[1:]:
        z_a[k].wait_recv()
    x_a = send(a.at[block_a], me.at(x_hi=1 - me.x_hi))
    core_a = [send(a.at[block_a], other)]
    turn(10, 14)
    for k in NEAR:
        to_x[k].wait_recv()
        ref = piece(me.y, 1 - me.x_lo, k)
        to_up[1, k] = send(ref, up)
        to_down[1, k] = send(ref, down)
    turn(14, 18)
    relayed = []
    for side in range(2):
        x_lo = me.x_lo if side == 0 else 1 - me.x_lo
        for k in NEAR:
            to_up[side, k].wait_recv()
            to_down[side, k].wait_recv()
            if k % 2 == 0:
                relayed.append(send(piece(below, x_lo, k), up))
            else:
                relayed.append(send(piece(above, x_lo, k), down))
        if side == 0:
            for copy in x_c:
                copy.wait_recv()
            core_c = []
            for lo_hi in range(4):
                core_c.append(send(c.at[:, lo_hi * 2 + me.core], other))
            x_a.wait_recv()
            core_a.append(send(a.at[(1 - me.x_hi) * 2 + me.core], other))
            turn(18, 22)
    turn(22, 24)
    for copy in core_a + core_c + relayed:
        copy.wait_recv()
    copies.drain()


def gather(fa, fb, fc, x):
    n = 7 + 7 + 3 + 8 * 3 + 3 + 2 + 8 * 2 + 16 + 4 + 1
    a, b, c, xt = pl.pallas_call(
        gather_kernel,
        out_shape=(
            jax.ShapeDtypeStruct((4, NZ, SHARD, R), BF16),
            jax.ShapeDtypeStruct((8, NZ, SHARD, R), BF16),
            jax.ShapeDtypeStruct((4, 8, SHARD, R), BF16),
            jax.ShapeDtypeStruct((SLOTS * CHUNKS, CHUNK, BLK, BLK), BF16),
        ),
        in_specs=[VMEM] * 3 + [pl.BlockSpec(memory_space=pl.ANY)],
        out_specs=(VMEM,) * 3 + (pl.BlockSpec(memory_space=pl.ANY),),
        scratch_shapes=[
            pltpu.VMEM((2, BLK, CHUNK, BLK), BF16),
            pltpu.VMEM((2, CHUNK, BLK, BLK), BF16),
            pltpu.VMEM((UNIT * CHUNK, UNIT * CHUNK), BF16),
            pltpu.SemaphoreType.DMA((n,)),
            pltpu.SemaphoreType.DMA((n,)),
            pltpu.SemaphoreType.DMA((3,)),
            pltpu.SemaphoreType.DMA((2,)),
            pltpu.SemaphoreType.DMA((2,)),
        ],
        compiler_params=pltpu.CompilerParams(collective_id=0, has_side_effects=True),
        name="gather",
    )(fa, fb, fc, x)
    return (
        a.reshape(512, R), b.reshape(1024, R), c.reshape(512, R), xt.reshape(SLOTS, BLK, BLK, BLK)
    )


def terms_kernel(
    coords, filled, x_ref, m_ref, a_ref, b_ref, c_ref, ga, gb, gc, acc_a, acc_c, pb, cf, kh_s, mis_s
):
    slot, chunk = pl.program_id(0), pl.program_id(1)

    @pl.when((slot == 0) & (chunk == 0))
    def _():
        ga[...] = jnp.zeros_like(ga)
        gb[...] = jnp.zeros_like(gb)
        gc[...] = jnp.zeros_like(gc)

    @pl.when(slot < filled[0])
    def _():
        start_a = pl.multiple_of(coords[0, 0, slot] * BLK, BLK)
        start_b = pl.multiple_of(coords[1, 0, slot] * BLK, BLK)
        start_c = pl.multiple_of(coords[2, 0, slot] * BLK, BLK)

        @pl.when(chunk == 0)
        def _():
            acc_a[...] = jnp.zeros_like(acc_a)
            acc_c[...] = jnp.zeros_like(acc_c)
            cf[...] = c_ref[pl.ds(start_c, BLK), :].astype(F32)

        rows_a = a_ref[pl.ds(start_a, BLK), :]
        rows_c = c_ref[pl.ds(start_c, BLK), :]
        first_b = pl.multiple_of(start_b + chunk * CHUNK, CHUNK)
        rows_b = b_ref[pl.ds(first_b, CHUNK), :].astype(F32)
        scale = pltpu.roll(m_ref[0].astype(F32) * (1.0 / BLK), (BLK - chunk * CHUNK) % BLK, 1)
        for first in range(0, CHUNK, NV):
            vs = range(first, first + NV)
            kh, mis = [], []
            for v in vs:
                row = jnp.broadcast_to(rows_b[v : v + 1, :], (16, R)).astype(BF16)
                kh.append((rows_c.reshape(8, 16, R) * row[None]).reshape(BLK, R))
            kh = jnp.concatenate(kh, 0)
            kh_s[BLK * first : BLK * (first + NV), :] = kh
            log_rate = lax.dot_general(
                rows_a, kh, (((1,), (1,)), ((), ())), preferred_element_type=F32
            )
            rate = jnp.exp(log_rate)
            for j, v in enumerate(vs):
                x = x_ref[0, v].astype(F32)
                w = scale[:, v : v + 1]
                mis.append((w * (rate[:, j * BLK : (j + 1) * BLK] - x)).astype(BF16))
            mis = jnp.concatenate(mis, 1)
            mis_s[:, BLK * first : BLK * (first + NV)] = mis
            folded = lax.dot_general(
                mis, rows_a, (((0,), (0,)), ((), ())), preferred_element_type=F32
            )
            folded = folded.astype(BF16).astype(F32)
            total = None
            for j, v in enumerate(vs):
                f = folded[j * BLK : (j + 1) * BLK]
                pb[v] = (f * cf[...]).reshape(16, 8, R).sum(0)
                part = f * rows_b[v : v + 1]
                total = part if total is None else total + part
            acc_c[...] += total
        acc_a[...] += jnp.dot(mis_s[...], kh_s[...], preferred_element_type=F32)
        gb[pl.ds(first_b, CHUNK), :] += pb[...].sum(1)

        @pl.when(chunk == CHUNKS - 1)
        def _():
            ga[pl.ds(start_a, BLK), :] += acc_a[...]
            gc[pl.ds(start_c, BLK), :] += acc_c[...]


def terms(blocks, fibers, coords, filled, a, b, c):
    def held(slot, filled):
        return jnp.minimum(slot, jnp.maximum(filled[0] - 1, 0))

    def x_block(slot, chunk, coords, filled):
        return (held(slot, filled), jnp.where(slot < filled[0], chunk, CHUNKS - 1), 0, 0)

    def m_block(slot, chunk, coords, filled):
        return (held(slot, filled), 0, 0)

    def whole(slot, chunk, coords, filled):
        return (0, 0)

    return pl.pallas_call(
        terms_kernel,
        out_shape=(
            jax.ShapeDtypeStruct((512, R), F32),
            jax.ShapeDtypeStruct((1024, R), F32),
            jax.ShapeDtypeStruct((512, R), F32),
        ),
        grid_spec=pltpu.PrefetchScalarGridSpec(
            num_scalar_prefetch=2,
            grid=(SLOTS, CHUNKS),
            in_specs=[
                pl.BlockSpec((1, CHUNK, BLK, BLK), x_block),
                pl.BlockSpec((1, BLK, BLK), m_block),
                pl.BlockSpec((512, R), whole),
                pl.BlockSpec((1024, R), whole),
                pl.BlockSpec((512, R), whole),
            ],
            out_specs=(
                pl.BlockSpec((512, R), whole),
                pl.BlockSpec((1024, R), whole),
                pl.BlockSpec((512, R), whole),
            ),
            scratch_shapes=[
                pltpu.VMEM((BLK, R), F32),
                pltpu.VMEM((BLK, R), F32),
                pltpu.VMEM((CHUNK, 8, R), F32),
                pltpu.VMEM((BLK, R), F32),
                pltpu.VMEM((CHUNK * BLK, R), BF16),
                pltpu.VMEM((BLK, CHUNK * BLK), BF16),
            ],
        ),
        name="terms",
    )(coords, filled, blocks, fibers, a, b, c)


def scatter_kernel(
    ga, gb, gc, out,
    a1, a2, a3, sa1, sa2, b1, b2, b3, d1, d2, d3, sb1, sb2, sd1, sd2, c1, c2, c3, sc1, sc2,
    send_sems, recv_sems,
):
    me = Place()
    copies = Copies(send_sems, recv_sems)
    me.greet()
    me.met()
    other = me.at(core=1 - me.core)
    left, right = slice(0, 128), slice(128, 256)
    in_b, in_d = [], []
    for k in range(1, NY):
        there = (me.y + k) % NY
        in_b.append(copies.start(gb.at[there, :, :, :, left], b1.at[k - 1], me.at(y=there)))
    to = 1 - me.x_lo
    for y in range(NY):
        in_d.append(copies.start(gb.at[y, to, :, :, right], d1.at[y], me.at(x_lo=to)))
    in_a = [
        copies.start(ga.at[hi, 1 - me.core], a1.at[hi], other) for hi in range(2)
    ]
    in_c = [copies.start(gc.at[:, 1 - me.core], c1, other)]
    for copy in in_a:
        copy.wait_recv()
    for hi in range(2):
        sa1[hi] = ga[hi, me.core] + a1[hi]
    in_a = [copies.start(sa1.at[1 - me.x_hi], a2, me.at(x_hi=1 - me.x_hi))]
    for copy in in_c:
        copy.wait_recv()
    sc1[...] = gc[:, me.core] + c1[...]
    in_c = []
    for k in range(1, NY):
        there = (me.y + k) % NY
        in_c.append(copies.start(sc1.at[pl.ds(there * 4, 4)], c2.at[k - 1], me.at(y=there)))
    for copy in in_d:
        copy.wait_recv()
    for y in range(NY):
        sd1[y] = gb[y, me.x_lo, :, :, right] + d1[y]
    in_d = []
    for k in range(1, NY):
        there = (me.y + k) % NY
        in_d.append(copies.start(sd1.at[there], d2.at[k - 1], me.at(y=there)))
    for copy in in_b:
        copy.wait_recv()
    sb1[...] = gb[me.y, :, :, :, left] + b1[0] + b1[1] + b1[2]
    in_b = [copies.start(sb1.at[to], b2, me.at(x_lo=to))]
    for copy in in_a:
        copy.wait_recv()
    sa2[...] = sa1[me.x_hi] + a2[...]
    in_a = []
    for k in range(1, NZ):
        there = (me.z + k) % NZ
        in_a.append(copies.start(sa2.at[there], a3.at[k - 1], me.at(z=there)))
    for copy in in_c:
        copy.wait_recv()
    sc2[...] = sc1[pl.ds(me.y * 4, 4)] + c2[0] + c2[1] + c2[2]
    in_c = []
    for k, (lo, hi) in enumerate(me.x_peers()):
        in_c.append(copies.start(sc2.at[lo * 2 + hi], c3.at[k], me.at(x_lo=lo, x_hi=hi)))
    for copy in in_d:
        copy.wait_recv()
    sd2[...] = sd1[me.y] + d2[0] + d2[1] + d2[2]
    in_d = []
    for k in range(1, NZ):
        there = (me.z + k) % NZ
        in_d.append(copies.start(sd2.at[there], d3.at[k - 1], me.at(z=there)))
    for copy in in_b:
        copy.wait_recv()
    sb2[...] = sb1[me.x_lo] + b2[...]
    in_b = []
    for k in range(1, NZ):
        there = (me.z + k) % NZ
        in_b.append(copies.start(sb2.at[there], b3.at[k - 1], me.at(z=there)))
    for copy in in_c:
        copy.wait_recv()
    out[2] = sc2[me.x_lo * 2 + me.x_hi] + c3[0] + c3[1] + c3[2]
    for copy in in_a:
        copy.wait_recv()
    out[0] = sa2[me.z] + a3[...].sum(0)
    for copy in in_d:
        copy.wait_recv()
    out[1, :, right] = sd2[me.z] + d3[...].sum(0)
    for copy in in_b:
        copy.wait_recv()
    out[1, :, left] = sb2[me.z] + b3[...].sum(0)
    copies.drain()


def scatter(ga, gb, gc):
    n = 3 + 4 + 2 + 1 + 1 + 3 + 3 + 1 + 7 + 3 + 7 + 7
    half = R // 2

    def buf(*shape):
        return pltpu.VMEM(shape, F32)

    out = pl.pallas_call(
        scatter_kernel,
        out_shape=jax.ShapeDtypeStruct((3, SHARD, R), F32),
        in_specs=[VMEM] * 3,
        out_specs=VMEM,
        scratch_shapes=[
            buf(2, NZ, SHARD, R), buf(NZ, SHARD, R), buf(7, SHARD, R),
            buf(2, NZ, SHARD, R), buf(NZ, SHARD, R),
            buf(3, 2, NZ, SHARD, half), buf(NZ, SHARD, half), buf(7, SHARD, half),
            buf(4, NZ, SHARD, half), buf(3, NZ, SHARD, half), buf(7, SHARD, half),
            buf(2, NZ, SHARD, half), buf(NZ, SHARD, half),
            buf(4, NZ, SHARD, half), buf(NZ, SHARD, half),
            buf(16, SHARD, R), buf(3, 4, SHARD, R), buf(3, SHARD, R),
            buf(16, SHARD, R), buf(4, SHARD, R),
            pltpu.SemaphoreType.DMA((n,)),
            pltpu.SemaphoreType.DMA((n,)),
        ],
        compiler_params=pltpu.CompilerParams(collective_id=1, has_side_effects=True),
        name="scatter",
    )(
        ga.reshape(2, 2, NZ, SHARD, R),
        gb.reshape(NY, 2, NZ, SHARD, R),
        gc.reshape(16, 2, SHARD, R),
    )
    return pl.pallas_call(
        part_kernel,
        out_shape=(jax.ShapeDtypeStruct((1, SHARD, R), F32),) * 3,
        in_specs=[VMEM],
        out_specs=(VMEM,) * 3,
        name="part",
    )(out)


def part_kernel(rows, a, b, c):
    for i, ref in enumerate((a, b, c)):
        ref[0] = rows[i]


def per_device(tensor_blocks, fiber_mask, block_coords, block_counts, factor_a, factor_b, factor_c):
    a, b, c, turned = gather(
        factor_a, factor_b, factor_c, tensor_blocks.reshape(SLOTS, BLK, BLK, BLK)
    )
    ga, gb, gc = terms(
        turned,
        fiber_mask.reshape(SLOTS, BLK, BLK),
        block_coords.reshape(3, 1, SLOTS),
        block_counts.reshape(1),
        a, b, c,
    )
    return scatter(ga, gb, gc)


def solution(mesh):
    placed = (
        P("gx", "gy", "gz", None, None, None, None),
        P("gx", "gy", "gz", None, None, None),
        P("gx", "gy", "gz", None, None),
        P("gx", "gy", "gz"),
        P("gx", ("gy", "gz"), None),
        P("gy", ("gx", "gz"), None),
        P("gz", ("gx", "gy"), None),
    )
    return jax.shard_map(
        per_device,
        mesh=mesh,
        in_specs=placed,
        out_specs=(
            P("gx", ("gy", "gz"), None),
            P("gy", ("gx", "gz"), None),
            P("gz", ("gx", "gy"), None),
        ),
        check_vma=False,
    )
```

```python
import functools

import jax
import jax.numpy as jnp
from jax import lax
from jax.experimental import pallas as pl
from jax.experimental.pallas import tpu as pltpu
from jax.sharding import PartitionSpec as P

R = 256
BLK = 128
SLOTS = 3
SHARD = 16
NX, NY, NZ = 2, 4, 8
CHUNK = 16
CHUNKS = BLK // CHUNK
NV = 8
VMEM_LIMIT = 50 << 20
DEPTH = 6
UNIT = 8
F32 = jnp.float32
BF16 = jnp.bfloat16
MESH = pl.DeviceIdType.MESH
VMEM = pl.BlockSpec(memory_space=pltpu.VMEM)


class Place:
    def __init__(self):
        gx, gy, gz = lax.axis_index("gx"), lax.axis_index("gy"), lax.axis_index("gz")
        self.y, self.x_lo = gx // 2, gx % 2
        self.x_hi, self.core = gy // 2, gy % 2
        self.z = gz

    def at(self, y=None, x_lo=None, x_hi=None, core=None, z=None):
        y = self.y if y is None else y
        x_lo = self.x_lo if x_lo is None else x_lo
        x_hi = self.x_hi if x_hi is None else x_hi
        core = self.core if core is None else core
        z = self.z if z is None else z
        return (y * 2 + x_lo, x_hi * 2 + core, z)

    def greet(self):
        barrier = pltpu.get_barrier_semaphore()
        peers = [self.at(core=1 - self.core)]
        peers += [self.at(z=(self.z + k) % NZ) for k in range(1, NZ)]
        peers += [self.at(y=(self.y + k) % NY) for k in range(1, NY)]
        peers += [self.at(x_lo=lo, x_hi=hi) for lo, hi in self.x_peers()]
        for peer in peers:
            pl.semaphore_signal(barrier, inc=1, device_id=peer, device_id_type=MESH)
        self.greeted = len(peers)

    def met(self):
        pl.semaphore_wait(pltpu.get_barrier_semaphore(), self.greeted)

    def x_peers(self):
        lo, hi = self.x_lo, self.x_hi
        return [(1 - lo, hi), (lo, 1 - hi), (1 - lo, 1 - hi)]


class Copies:
    def __init__(self, send_sems, recv_sems):
        self.send_sems, self.recv_sems = send_sems, recv_sems
        self.n = 0
        self.started = []

    def start(self, src, dst, peer):
        copy = pltpu.make_async_remote_copy(
            src_ref=src,
            dst_ref=dst,
            send_sem=self.send_sems.at[self.n],
            recv_sem=self.recv_sems.at[self.n],
            device_id=peer,
            device_id_type=MESH,
        )
        self.n += 1
        copy.start()
        self.started.append(copy)
        return copy

    def drain(self):
        for copy in self.started:
            copy.wait_send()


def turn_chunks(lo, hi, x, xt, xin, xout, perm, in_sems, out_sems):
    def source(i):
        return x.at[i // CHUNKS, :, pl.ds(pl.multiple_of(i % CHUNKS * CHUNK, CHUNK), CHUNK), :]

    def load(i):
        return pltpu.make_async_copy(source(i), xin.at[i % DEPTH], in_sems.at[i % DEPTH])

    def store(i):
        return pltpu.make_async_copy(xout.at[i % DEPTH], xt.at[i], out_sems.at[i % DEPTH])

    if lo == 0:
        for i in range(DEPTH - 1):
            load(i).start()

    def body(i, carry):
        load(i).wait()

        @pl.when(i <= SLOTS * CHUNKS - DEPTH)
        def _():
            load(i + DEPTH - 1).start()

        @pl.when(i >= DEPTH)
        def _():
            store(i - DEPTH).wait()

        for g in range(BLK // UNIT):
            us = slice(UNIT * g, UNIT * g + UNIT)
            rows = xin[i % DEPTH, us].reshape(UNIT * CHUNK, BLK)
            rows = jnp.dot(perm[...], rows, preferred_element_type=F32).astype(BF16)
            xout[i % DEPTH, :, us, :] = rows.reshape(CHUNK, UNIT, BLK)
        store(i).start()
        return carry

    lax.fori_loop(lo, hi, body, 0)
    if hi == SLOTS * CHUNKS:
        for i in range(hi - DEPTH, hi):
            store(i).wait()


NEAR = (0, 7, 1, 6, 2, 5, 3, 4)


def gather_kernel(
    fa, fb, fc, x, a, b, c, xt, xin, xout, perm, send_sems, recv_sems, own_sems, in_sems, out_sems
):
    me = Place()
    copies = Copies(send_sems, recv_sems)
    turn = functools.partial(
        turn_chunks, x=x, xt=xt, xin=xin, xout=xout, perm=perm, in_sems=in_sems, out_sems=out_sems
    )
    block_a = me.x_hi * 2 + me.core
    block_b = me.y * 2 + me.x_lo
    block_c = (me.x_lo * 2 + me.x_hi) * 2 + me.core
    own = [
        pltpu.make_async_copy(fb.at[0], b.at[block_b, me.z], own_sems.at[0]),
        pltpu.make_async_copy(fa.at[0], a.at[block_a, me.z], own_sems.at[1]),
        pltpu.make_async_copy(fc.at[0], c.at[me.y, block_c], own_sems.at[2]),
    ]
    for copy in own:
        copy.start()
    me.greet()
    row = lax.broadcasted_iota(jnp.int32, perm.shape, 0)
    col = lax.broadcasted_iota(jnp.int32, perm.shape, 1)
    swapped = (row % UNIT) * CHUNK + row // UNIT
    perm[...] = jnp.where(col == swapped, 1.0, 0.0).astype(BF16)
    turn(0, 4)
    for copy in own:
        copy.wait()
    me.met()
    z_b, z_a, y_c = {}, {}, []
    for k in reversed(NEAR[1:]):
        z_b[k] = copies.start(b.at[block_b, me.z], b.at[block_b, me.z], me.at(z=(me.z + k) % NZ))
    for k in range(1, NY):
        y_c.append(copies.start(c.at[me.y, block_c], c.at[me.y, block_c], me.at(y=(me.y + k) % NY)))
    for k in reversed(NEAR[1:]):
        z_a[k] = copies.start(a.at[block_a, me.z], a.at[block_a, me.z], me.at(z=(me.z + k) % NZ))
    up, down = me.at(y=(me.y + 1) % NY), me.at(y=(me.y + NY - 1) % NY)
    above, below = (me.y + 1) % NY, (me.y + NY - 1) % NY
    beside = me.at(x_lo=1 - me.x_lo)

    def piece(y, x_lo, k):
        return b.at[y * 2 + x_lo, (me.z + NZ - k) % NZ]

    def send(ref, peer):
        return copies.start(ref, ref, peer)

    to_x, to_up, to_down = {}, {}, {}

    def spread(k):
        if k:
            z_b[k].wait_recv()
        ref = piece(me.y, me.x_lo, k)
        to_x[k] = send(ref, beside)
        to_up[0, k] = send(ref, up)
        to_down[0, k] = send(ref, down)

    spread(0)
    turn(4, 10)
    for k in NEAR[1:]:
        spread(k)
    for copy in y_c:
        copy.wait_recv()
    part_c = c.at[:, block_c]
    x_c = [send(part_c, me.at(x_lo=lo, x_hi=hi)) for lo, hi in me.x_peers()]
    other = me.at(core=1 - me.core)
    for k in NEAR[1:]:
        z_a[k].wait_recv()
    x_a = send(a.at[block_a], me.at(x_hi=1 - me.x_hi))
    core_a = [send(a.at[block_a], other)]
    turn(10, 14)
    for k in NEAR:
        to_x[k].wait_recv()
        ref = piece(me.y, 1 - me.x_lo, k)
        to_up[1, k] = send(ref, up)
        to_down[1, k] = send(ref, down)
    turn(14, 18)
    relayed = []
    for side in range(2):
        x_lo = me.x_lo if side == 0 else 1 - me.x_lo
        for k in NEAR:
            to_up[side, k].wait_recv()
            to_down[side, k].wait_recv()
            if k % 2 == 0:
                relayed.append(send(piece(below, x_lo, k), up))
            else:
                relayed.append(send(piece(above, x_lo, k), down))
        if side == 0:
            for copy in x_c:
                copy.wait_recv()
            core_c = []
            for lo_hi in range(4):
                core_c.append(send(c.at[:, lo_hi * 2 + me.core], other))
            x_a.wait_recv()
            core_a.append(send(a.at[(1 - me.x_hi) * 2 + me.core], other))
            turn(18, 22)
    turn(22, 24)
    for copy in core_a + core_c + relayed:
        copy.wait_recv()
    copies.drain()


def gather(fa, fb, fc, x):
    n = 7 + 7 + 3 + 8 * 3 + 3 + 2 + 8 * 2 + 16 + 4 + 1
    a, b, c, xt = pl.pallas_call(
        gather_kernel,
        out_shape=(
            jax.ShapeDtypeStruct((4, NZ, SHARD, R), BF16),
            jax.ShapeDtypeStruct((8, NZ, SHARD, R), BF16),
            jax.ShapeDtypeStruct((4, 8, SHARD, R), BF16),
            jax.ShapeDtypeStruct((SLOTS * CHUNKS, CHUNK, BLK, BLK), BF16),
        ),
        in_specs=[pl.BlockSpec(memory_space=pl.ANY)] * 4,
        out_specs=(VMEM,) * 3 + (pl.BlockSpec(memory_space=pl.ANY),),
        scratch_shapes=[
            pltpu.VMEM((DEPTH, BLK, CHUNK, BLK), BF16),
            pltpu.VMEM((DEPTH, CHUNK, BLK, BLK), BF16),
            pltpu.VMEM((UNIT * CHUNK, UNIT * CHUNK), BF16),
            pltpu.SemaphoreType.DMA((n,)),
            pltpu.SemaphoreType.DMA((n,)),
            pltpu.SemaphoreType.DMA((3,)),
            pltpu.SemaphoreType.DMA((DEPTH,)),
            pltpu.SemaphoreType.DMA((DEPTH,)),
        ],
        compiler_params=pltpu.CompilerParams(
            collective_id=0, has_side_effects=True, vmem_limit_bytes=VMEM_LIMIT
        ),
        name="gather",
    )(*(pltpu.with_memory_space_constraint(arg, pltpu.HBM) for arg in (fa, fb, fc, x)))
    return (
        a.reshape(512, R), b.reshape(1024, R), c.reshape(512, R), xt.reshape(SLOTS, BLK, BLK, BLK)
    )


def terms_kernel(
    coords, filled, x_ref, m_ref, a_ref, b_ref, c_ref, ga, gb, gc, acc_a, acc_c, pb, cf, kh_s, mis_s
):
    slot, chunk = pl.program_id(0), pl.program_id(1)

    @pl.when((slot == 0) & (chunk == 0))
    def _():
        ga[...] = jnp.zeros_like(ga)
        gb[...] = jnp.zeros_like(gb)
        gc[...] = jnp.zeros_like(gc)

    @pl.when(slot < filled[0, 0, 0])
    def _():
        start_a = pl.multiple_of(coords[0, 0, slot] * BLK, BLK)
        start_b = pl.multiple_of(coords[1, 0, slot] * BLK, BLK)
        start_c = pl.multiple_of(coords[2, 0, slot] * BLK, BLK)

        @pl.when(chunk == 0)
        def _():
            acc_a[...] = jnp.zeros_like(acc_a)
            acc_c[...] = jnp.zeros_like(acc_c)
            cf[...] = c_ref[pl.ds(start_c, BLK), :].astype(F32)

        rows_a = a_ref[pl.ds(start_a, BLK), :]
        rows_c = c_ref[pl.ds(start_c, BLK), :]
        first_b = pl.multiple_of(start_b + chunk * CHUNK, CHUNK)
        rows_b = b_ref[pl.ds(first_b, CHUNK), :].astype(F32)
        scale = pltpu.roll(m_ref[0].astype(F32) * (1.0 / BLK), (BLK - chunk * CHUNK) % BLK, 1)
        for first in range(0, CHUNK, NV):
            vs = range(first, first + NV)
            kh, mis = [], []
            for v in vs:
                row = jnp.broadcast_to(rows_b[v : v + 1, :], (16, R)).astype(BF16)
                kh.append((rows_c.reshape(8, 16, R) * row[None]).reshape(BLK, R))
            kh = jnp.concatenate(kh, 0)
            kh_s[BLK * first : BLK * (first + NV), :] = kh
            log_rate = lax.dot_general(
                rows_a, kh, (((1,), (1,)), ((), ())), preferred_element_type=F32
            )
            rate = jnp.exp(log_rate)
            for j, v in enumerate(vs):
                x = x_ref[0, v].astype(F32)
                w = scale[:, v : v + 1]
                mis.append((w * (rate[:, j * BLK : (j + 1) * BLK] - x)).astype(BF16))
            mis = jnp.concatenate(mis, 1)
            mis_s[:, BLK * first : BLK * (first + NV)] = mis
            folded = lax.dot_general(
                mis, rows_a, (((0,), (0,)), ((), ())), preferred_element_type=F32
            )
            folded = folded.astype(BF16).astype(F32)
            total = None
            for j, v in enumerate(vs):
                f = folded[j * BLK : (j + 1) * BLK]
                pb[v] = (f * cf[...]).reshape(16, 8, R).sum(0)
                part = f * rows_b[v : v + 1]
                total = part if total is None else total + part
            acc_c[...] += total
        acc_a[...] += jnp.dot(mis_s[...], kh_s[...], preferred_element_type=F32)
        gb[pl.ds(first_b, CHUNK), :] += pb[...].sum(1)

        @pl.when(chunk == CHUNKS - 1)
        def _():
            ga[pl.ds(start_a, BLK), :] += acc_a[...]
            gc[pl.ds(start_c, BLK), :] += acc_c[...]


def terms(blocks, fibers, coords, filled, a, b, c):
    def x_block(slot, chunk, coords):
        return (slot, chunk, 0, 0)

    def m_block(slot, chunk, coords):
        return (slot, 0, 0)

    def whole(slot, chunk, coords):
        return (0, 0)

    return pl.pallas_call(
        terms_kernel,
        out_shape=(
            jax.ShapeDtypeStruct((512, R), F32),
            jax.ShapeDtypeStruct((1024, R), F32),
            jax.ShapeDtypeStruct((512, R), F32),
        ),
        grid_spec=pltpu.PrefetchScalarGridSpec(
            num_scalar_prefetch=1,
            grid=(SLOTS, CHUNKS),
            in_specs=[
                pl.BlockSpec(memory_space=pltpu.SMEM),
                pl.BlockSpec((1, CHUNK, BLK, BLK), x_block),
                pl.BlockSpec((1, BLK, BLK), m_block),
                pl.BlockSpec((512, R), whole),
                pl.BlockSpec((1024, R), whole),
                pl.BlockSpec((512, R), whole),
            ],
            out_specs=(
                pl.BlockSpec((512, R), whole),
                pl.BlockSpec((1024, R), whole),
                pl.BlockSpec((512, R), whole),
            ),
            scratch_shapes=[
                pltpu.VMEM((BLK, R), F32),
                pltpu.VMEM((BLK, R), F32),
                pltpu.VMEM((CHUNK, 8, R), F32),
                pltpu.VMEM((BLK, R), F32),
                pltpu.VMEM((CHUNK * BLK, R), BF16),
                pltpu.VMEM((BLK, CHUNK * BLK), BF16),
            ],
        ),
        compiler_params=pltpu.CompilerParams(vmem_limit_bytes=VMEM_LIMIT),
        name="terms",
    )(coords, filled, blocks, fibers, a, b, c)


def scatter_kernel(
    ga, gb, gc, out,
    a1, a2, a3, sa1, sa2, b1, b2, b3, d1, d2, d3, sb1, sb2, sd1, sd2, c1, c2, c3, sc1, sc2,
    send_sems, recv_sems,
):
    me = Place()
    copies = Copies(send_sems, recv_sems)
    me.greet()
    me.met()
    other = me.at(core=1 - me.core)
    left, right = slice(0, 128), slice(128, 256)
    in_b, in_d = [], []
    for k in range(1, NY):
        there = (me.y + k) % NY
        in_b.append(copies.start(gb.at[there, :, :, :, left], b1.at[k - 1], me.at(y=there)))
    to = 1 - me.x_lo
    for y in range(NY):
        in_d.append(copies.start(gb.at[y, to, :, :, right], d1.at[y], me.at(x_lo=to)))
    in_a = [
        copies.start(ga.at[hi, 1 - me.core], a1.at[hi], other) for hi in range(2)
    ]
    in_c = [copies.start(gc.at[:, 1 - me.core], c1, other)]
    for copy in in_a:
        copy.wait_recv()
    for hi in range(2):
        sa1[hi] = ga[hi, me.core] + a1[hi]
    in_a = [copies.start(sa1.at[1 - me.x_hi], a2, me.at(x_hi=1 - me.x_hi))]
    for copy in in_c:
        copy.wait_recv()
    sc1[...] = gc[:, me.core] + c1[...]
    in_c = []
    for k in range(1, NY):
        there = (me.y + k) % NY
        in_c.append(copies.start(sc1.at[pl.ds(there * 4, 4)], c2.at[k - 1], me.at(y=there)))
    for copy in in_d:
        copy.wait_recv()
    for y in range(NY):
        sd1[y] = gb[y, me.x_lo, :, :, right] + d1[y]
    in_d = []
    for k in range(1, NY):
        there = (me.y + k) % NY
        in_d.append(copies.start(sd1.at[there], d2.at[k - 1], me.at(y=there)))
    for copy in in_b:
        copy.wait_recv()
    sb1[...] = gb[me.y, :, :, :, left] + b1[0] + b1[1] + b1[2]
    in_b = [copies.start(sb1.at[to], b2, me.at(x_lo=to))]
    for copy in in_a:
        copy.wait_recv()
    sa2[...] = sa1[me.x_hi] + a2[...]
    in_a = []
    for k in range(1, NZ):
        there = (me.z + k) % NZ
        in_a.append(copies.start(sa2.at[there], a3.at[k - 1], me.at(z=there)))
    for copy in in_c:
        copy.wait_recv()
    sc2[...] = sc1[pl.ds(me.y * 4, 4)] + c2[0] + c2[1] + c2[2]
    in_c = []
    for k, (lo, hi) in enumerate(me.x_peers()):
        in_c.append(copies.start(sc2.at[lo * 2 + hi], c3.at[k], me.at(x_lo=lo, x_hi=hi)))
    for copy in in_d:
        copy.wait_recv()
    sd2[...] = sd1[me.y] + d2[0] + d2[1] + d2[2]
    in_d = []
    for k in range(1, NZ):
        there = (me.z + k) % NZ
        in_d.append(copies.start(sd2.at[there], d3.at[k - 1], me.at(z=there)))
    for copy in in_b:
        copy.wait_recv()
    sb2[...] = sb1[me.x_lo] + b2[...]
    in_b = []
    for k in range(1, NZ):
        there = (me.z + k) % NZ
        in_b.append(copies.start(sb2.at[there], b3.at[k - 1], me.at(z=there)))
    for copy in in_c:
        copy.wait_recv()
    out[2] = sc2[me.x_lo * 2 + me.x_hi] + c3[0] + c3[1] + c3[2]
    for copy in in_a:
        copy.wait_recv()
    out[0] = sa2[me.z] + a3[...].sum(0)
    for copy in in_d:
        copy.wait_recv()
    out[1, :, right] = sd2[me.z] + d3[...].sum(0)
    for copy in in_b:
        copy.wait_recv()
    out[1, :, left] = sb2[me.z] + b3[...].sum(0)
    copies.drain()


def scatter(ga, gb, gc):
    n = 3 + 4 + 2 + 1 + 1 + 3 + 3 + 1 + 7 + 3 + 7 + 7
    half = R // 2

    def buf(*shape):
        return pltpu.VMEM(shape, F32)

    out = pl.pallas_call(
        scatter_kernel,
        out_shape=jax.ShapeDtypeStruct((3, SHARD, R), F32),
        in_specs=[VMEM] * 3,
        out_specs=VMEM,
        scratch_shapes=[
            buf(2, NZ, SHARD, R), buf(NZ, SHARD, R), buf(7, SHARD, R),
            buf(2, NZ, SHARD, R), buf(NZ, SHARD, R),
            buf(3, 2, NZ, SHARD, half), buf(NZ, SHARD, half), buf(7, SHARD, half),
            buf(4, NZ, SHARD, half), buf(3, NZ, SHARD, half), buf(7, SHARD, half),
            buf(2, NZ, SHARD, half), buf(NZ, SHARD, half),
            buf(4, NZ, SHARD, half), buf(NZ, SHARD, half),
            buf(16, SHARD, R), buf(3, 4, SHARD, R), buf(3, SHARD, R),
            buf(16, SHARD, R), buf(4, SHARD, R),
            pltpu.SemaphoreType.DMA((n,)),
            pltpu.SemaphoreType.DMA((n,)),
        ],
        compiler_params=pltpu.CompilerParams(
            collective_id=1, has_side_effects=True, vmem_limit_bytes=VMEM_LIMIT
        ),
        name="scatter",
    )(
        ga.reshape(2, 2, NZ, SHARD, R),
        gb.reshape(NY, 2, NZ, SHARD, R),
        gc.reshape(16, 2, SHARD, R),
    )
    return pl.pallas_call(
        part_kernel,
        out_shape=(jax.ShapeDtypeStruct((1, SHARD, R), F32),) * 3,
        in_specs=[VMEM],
        out_specs=(VMEM,) * 3,
        compiler_params=pltpu.CompilerParams(vmem_limit_bytes=VMEM_LIMIT),
        name="part",
    )(out)


def part_kernel(rows, a, b, c):
    for i, ref in enumerate((a, b, c)):
        ref[0] = rows[i]


def per_device(tensor_blocks, fiber_mask, block_coords, block_counts, factor_a, factor_b, factor_c):
    a, b, c, turned = gather(
        factor_a, factor_b, factor_c, tensor_blocks.reshape(SLOTS, BLK, BLK, BLK)
    )
    ga, gb, gc = terms(
        turned,
        fiber_mask.reshape(SLOTS, BLK, BLK),
        block_coords.reshape(3, 1, SLOTS),
        block_counts,
        a, b, c,
    )
    return scatter(ga, gb, gc)


def solution(mesh):
    placed = (
        P("gx", "gy", "gz", None, None, None, None),
        P("gx", "gy", "gz", None, None, None),
        P("gx", "gy", "gz", None, None),
        P("gx", "gy", "gz"),
        P("gx", ("gy", "gz"), None),
        P("gy", ("gx", "gz"), None),
        P("gz", ("gx", "gy"), None),
    )
    return jax.shard_map(
        per_device,
        mesh=mesh,
        in_specs=placed,
        out_specs=(
            P("gx", ("gy", "gz"), None),
            P("gy", ("gx", "gz"), None),
            P("gz", ("gx", "gy"), None),
        ),
        check_vma=False,
    )
```
